32 devices in a mesh: dp: 8 (over z, y), seq: 4 (over x, core).
Axes of the slice: x: 2, y: 2, z: 4, core: 2. Of those that a mesh axis runs over, the one named last changes fastest.
Arguments:
- tokens: bfloat16 [128, 1024, 1280], P('dp', 'seq'), may hold values from -6 to 6
- cotangent: bfloat16 [128, 1024, 1280], P('dp', 'seq'), may hold values from -6 to 6
- ln1_gain: bfloat16 [1280], replicated, may hold values from 0.25 to 1.75
- ln1_bias: bfloat16 [1280], replicated, may hold values from -3 to 3
- w_in: bfloat16 [1280, 640], replicated, may hold values from -0.15625 to 0.15625
- b_in: bfloat16 [640], replicated, may hold values from -3 to 3
- ln2_gain: bfloat16 [640], replicated, may hold values from 0.25 to 1.75
- ln2_bias: bfloat16 [640], replicated, may hold values from -3 to 3
- w_conv: bfloat16 [5, 640, 640], replicated, may hold values from -0.109375 to 0.109375
- b_conv: bfloat16 [640], replicated, may hold values from -3 to 3
- ln3_gain: bfloat16 [640], replicated, may hold values from 0.25 to 1.75
- ln3_bias: bfloat16 [640], replicated, may hold values from -3 to 3
- w_out: bfloat16 [640, 1280], replicated, may hold values from -0.3125 to 0.3125
- b_out: bfloat16 [1280], replicated, may hold values from -3 to 3
- lengths: int32 [128], P('dp'), may hold values from 64 to 1024, as said below
- offsets: int32 [128], P('dp'), may hold values from 0 to 960, as said below
- live: int32 [8], P('dp'), may hold values from 8 to 16, as said below
Outputs:
- output: bfloat16 [128, 1024, 1280], P('dp', 'seq')
- grad_tokens: bfloat16 [128, 1024, 1280], P('dp', 'seq')
- grad_ln1_gain: float32 [1280], replicated
- grad_ln1_bias: float32 [1280], replicated
- grad_w_in: float32 [1280, 640], replicated
- grad_b_in: float32 [640], replicated
- grad_ln2_gain: float32 [640], replicated
- grad_ln2_bias: float32 [640], replicated
- grad_w_conv: float32 [5, 640, 640], replicated
- grad_b_conv: float32 [640], replicated
- grad_ln3_gain: float32 [640], replicated
- grad_ln3_bias: float32 [640], replicated
- grad_w_out: float32 [640, 1280], replicated
- grad_b_out: float32 [1280], replicated
The draws below stay inside these ranges and needn't reach their ends.
Inputs may be any that keep to these rules, and one draw needn't show every extreme that they name: offsets[s] + lengths[s] <= 1024. offsets[s] + lengths[s] <= 1024. Group g holds sequences in its slots 0 .. live[g] - 1; some group has all 16 slots filled.
All inputs are finite; a program needn't handle non-finite values.
Results may differ from the reference program's by a relative error of at most 0.0074.
Values may be sent and summed in bfloat16 or wider, within the bound.
A program may use at most 384 MiB of HBM per device.

```python
import jax
import jax.numpy as jnp
from jax import lax

D = 1280
INNER = 640
KERNEL_TAPS = 5
DILATION_STEP = 128
SLOT_POSITIONS = 1024
LEAST = 64
SLOT_DEV = 16
SLOTS = 128
GROUPS = 8


def crop_windows(key):
    base_key = jax.random.fold_in(key, 11)
    key_len, key_cut, key_pos = jax.random.split(base_key, 3)
    slot_ids = jnp.arange(SLOTS, dtype=jnp.int32)
    short_len = jax.random.randint(key_len, (SLOTS,), LEAST, SLOT_POSITIONS + 1, dtype=jnp.int32)
    cropped = (jax.random.randint(key_cut, (SLOTS,), 0, 2, dtype=jnp.int32) == 0) | (slot_ids == 0)
    seq_len = jnp.where(cropped, SLOT_POSITIONS, short_len)
    seq_len = jnp.where(slot_ids == SLOTS - 1, LEAST, seq_len)
    room_left = SLOT_POSITIONS - seq_len + 1
    start_pos = jax.random.randint(key_pos, (SLOTS,), 0, 1 << 20, dtype=jnp.int32) % room_left
    start_pos = jnp.where(slot_ids == SLOTS - 1, SLOT_POSITIONS - LEAST, start_pos)
    return (seq_len.astype(jnp.int32), start_pos.astype(jnp.int32))


def draw_lengths(key, part):
    return crop_windows(key)[0]


def draw_offsets(key, part):
    return crop_windows(key)[1]


def draw_live(key, part):
    key_count, key_full = jax.random.split(jax.random.fold_in(key, 23))
    counts = jax.random.randint(key_count, (GROUPS,), SLOT_DEV // 2, SLOT_DEV + 1, dtype=jnp.int32)
    full_group = jax.random.randint(key_full, (), 0, GROUPS, dtype=jnp.int32)
    return jnp.where(jnp.arange(GROUPS, dtype=jnp.int32) == full_group, SLOT_DEV, counts).astype(jnp.int32)


def block_scale(key, dims, pieces, least, largest):
    def one(dim, parts):
        steps = jax.random.uniform(jax.random.fold_in(jax.random.fold_in(key, 6), dim), (parts,), jnp.float32, least / len(pieces), largest / len(pieces))
        return jnp.repeat(jnp.exp(steps), dims[dim] // parts).reshape((-1,) + (1,) * (len(dims) - dim - 1))

    level = one(*pieces[0])
    for cut in pieces[1:]:
        level = level * one(*cut)
    return level


def noise(own_key, extent, deviation, limit, pieces=(), kind=jnp.bfloat16):
    loudness = block_scale(own_key, extent, pieces, -0.22, 0.18) if pieces else 1.0
    entries = jax.random.normal(own_key, extent, jnp.float32) * deviation * loudness
    return jnp.minimum(jnp.maximum(entries, -limit), limit).astype(kind)


def setup_inputs(seed: int = 0) -> dict:
    seeds = jax.random.split(jax.random.key(seed), 18)
    return {
        "tokens": noise(seeds[0], (SLOTS, SLOT_POSITIONS, D), 1.0, 6.0, ((0, 8), (1, 4))),
        "cotangent": noise(seeds[1], (SLOTS, SLOT_POSITIONS, D), 1.0, 6.0, ((0, 8), (1, 4))),
        "ln1_gain": jnp.clip(1.0 + 0.15 * jax.random.normal(seeds[2], (D,), jnp.float32), 0.25, 1.75).astype(jnp.bfloat16),
        "ln1_bias": noise(seeds[3], (D,), 0.5, 3.0),
        "w_in": noise(seeds[4], (D, INNER), D ** -0.5, 0.15625),
        "b_in": noise(seeds[5], (INNER,), 0.5, 3.0),
        "ln2_gain": jnp.clip(1.0 + 0.15 * jax.random.normal(seeds[6], (INNER,), jnp.float32), 0.25, 1.75).astype(jnp.bfloat16),
        "ln2_bias": noise(seeds[7], (INNER,), 0.5, 3.0),
        "w_conv": noise(seeds[8], (KERNEL_TAPS, INNER, INNER), (KERNEL_TAPS * INNER) ** -0.5, 0.109375),
        "b_conv": noise(seeds[9], (INNER,), 0.5, 3.0),
        "ln3_gain": jnp.clip(1.0 + 0.15 * jax.random.normal(seeds[10], (INNER,), jnp.float32), 0.25, 1.75).astype(jnp.bfloat16),
        "ln3_bias": noise(seeds[11], (INNER,), 0.5, 3.0),
        "w_out": noise(seeds[12], (INNER, D), (INNER // 2) ** -0.5, 0.3125),
        "b_out": noise(seeds[13], (D,), 0.5, 3.0),
        "lengths": draw_lengths(jax.random.fold_in(seeds[17], 71), 0),
        "offsets": draw_offsets(jax.random.fold_in(seeds[17], 71), 0),
        "live": draw_live(jax.random.fold_in(seeds[17], 71), 0),
    }


EPSILON = 1e-05

@jax.custom_vjp
def low(v):
    return lax.optimization_barrier(v.astype(jnp.bfloat16)).astype(jnp.float32)

@jax.custom_vjp
def low_back(v):
    return v

def low_keep(v):
    return (low(v), None)

def low_pass(kept, grad):
    return (grad,)

def back_keep(v):
    return (v, None)

def back_low(kept, grad):
    return (low(grad),)
low.defvjp(low_keep, low_pass)
low_back.defvjp(back_keep, back_low)

def layer_norm(values, gain, bias_vec):
    centre = values - lax.optimization_barrier(jnp.mean(values, axis=-1, keepdims=True))
    spread = lax.optimization_barrier(jnp.mean(centre * centre, axis=-1, keepdims=True))
    return centre * lax.rsqrt(spread + EPSILON) * gain + bias_vec

def gelu_exact(values):
    return jax.nn.gelu(values, approximate=False)

def project(values, weight):
    return jnp.einsum('spi,io->spo', values, weight, precision=lax.Precision.HIGHEST)

def dilated(inputs, weight, bias_vec):
    receptive_rows = (KERNEL_TAPS - 1) // 2 * DILATION_STEP
    padded_tokens = jnp.pad(inputs, ((0, 0), (receptive_rows, receptive_rows), (0, 0)))
    summed = bias_vec
    for kernel_tap_index in range(KERNEL_TAPS):
        shifted_window = padded_tokens[:, kernel_tap_index * DILATION_STEP:kernel_tap_index * DILATION_STEP + SLOT_POSITIONS]
        summed = summed + project(shifted_window, weight[kernel_tap_index])
    return summed

def block(inputs, keep_mask, ln1_gain, ln1_bias, w_in, b_in, ln2_gain, ln2_bias, w_conv, b_conv, ln3_gain, ln3_bias, w_out, b_out):
    first_act = gelu_exact(layer_norm(inputs, ln1_gain, ln1_bias))
    hidden = low_back(project(low(first_act), w_in) + b_in)
    conv_in = low_back(low(gelu_exact(layer_norm(hidden, ln2_gain, ln2_bias)))) * keep_mask[..., None]
    conv_out = low_back(low(dilated(conv_in, w_conv, b_conv)))
    last_act = gelu_exact(layer_norm(conv_out, ln3_gain, ln3_bias))
    return inputs + project(low(last_act), w_out) + b_out

def reference(tokens, cotangent, ln1_gain, ln1_bias, w_in, b_in, ln2_gain, ln2_bias, w_conv, b_conv, ln3_gain, ln3_bias, w_out, b_out, lengths, offsets, live):
    weights = tuple((array_item.astype(jnp.float32) for array_item in (ln1_gain, ln1_bias, w_in, b_in, ln2_gain, ln2_bias, w_conv, b_conv, ln3_gain, ln3_bias, w_out, b_out)))
    places = jnp.arange(SLOT_POSITIONS, dtype=jnp.int32)
    slot_ids = jnp.arange(SLOTS, dtype=jnp.int32)
    filled = slot_ids % SLOT_DEV < live[slot_ids // SLOT_DEV]
    inside = (places[None, :] >= offsets[:, None]) & (places[None, :] < (offsets + lengths)[:, None])
    keep_mask = (inside & filled[:, None]).astype(jnp.float32)
    group_size = 4
    batches = SLOTS // group_size
    token_groups = tokens.reshape(batches, group_size, SLOT_POSITIONS, D)
    cot_groups = cotangent.reshape(batches, group_size, SLOT_POSITIONS, D)
    mask_groups = keep_mask.reshape(batches, group_size, SLOT_POSITIONS)

    def one_group(totals, group_item):
        group_tokens, group_cot, group_mask = group_item

        def forward(inputs, *params):
            return block(inputs, group_mask, *params)
        result, pullback = jax.vjp(forward, group_tokens.astype(jnp.float32), *weights)
        gradients = pullback(group_cot.astype(jnp.float32) * group_mask[..., None])
        totals = tuple((summed + grad_term for summed, grad_term in zip(totals, gradients[1:])))
        return (totals, (result.astype(jnp.bfloat16), gradients[0].astype(jnp.bfloat16)))
    zero_grads = tuple((jnp.zeros(array_item.shape, jnp.float32) for array_item in weights))
    totals, (outputs, input_grads) = lax.scan(one_group, zero_grads, (token_groups, cot_groups, mask_groups))
    return (outputs.reshape(SLOTS, SLOT_POSITIONS, D), input_grads.reshape(SLOTS, SLOT_POSITIONS, D), totals[0], totals[1], totals[2], totals[3], totals[4], totals[5], totals[6], totals[7], totals[8], totals[9], totals[10], totals[11])
```

```python
import functools

import jax
import jax.numpy as jnp
from jax import lax
from jax.experimental import pallas as pl
from jax.experimental.pallas import tpu as pltpu
from jax.sharding import PartitionSpec as P

TAPS = 5
STEP = 128
REACH = (TAPS - 1) // 2 * STEP
EPSILON = 1e-05
SQRT_HALF = 0.7071067811865476
INV_ROOT_TAU = 0.3989422804014327
VMEM_LIMIT = 60 * 1024 * 1024
F32 = jnp.float32
BF16 = jnp.bfloat16


def dot(left, right):
    return jnp.dot(left, right, preferred_element_type=F32)


def dot_back(left, right):
    return lax.dot_general(left, right, (((1,), (1,)), ((), ())), preferred_element_type=F32)


def dot_rows(left, right):
    return lax.dot_general(left, right, (((0,), (0,)), ((), ())), preferred_element_type=F32)


def normalize(values):
    centre = values - jnp.mean(values, axis=-1, keepdims=True)
    inv = lax.rsqrt(jnp.mean(centre * centre, axis=-1, keepdims=True) + EPSILON)
    return centre * inv, inv


def gelu_pair(values):
    gate = 0.5 + 0.5 * lax.erf(values * SQRT_HALF)
    slope = gate + values * (INV_ROOT_TAU * jnp.exp(-0.5 * values * values))
    return values * gate, slope


def norm_back(grad, normed, inv, gain):
    scaled = grad * gain
    return inv * (
        scaled
        - jnp.mean(scaled, axis=-1, keepdims=True)
        - normed * jnp.mean(scaled * normed, axis=-1, keepdims=True)
    )


def keep_rows(win_ref, slot, shape):
    rows = lax.broadcasted_iota(jnp.int32, shape, 0)
    return (rows >= win_ref[0, slot]) & (rows < win_ref[1, slot])


def row_sum(values):
    return jnp.sum(values, axis=0, keepdims=True)


def spread(inv):
    return jnp.broadcast_to(inv, (inv.shape[0], 128))


def front_kernel(base, win, tok, g1, b1, w_in, b_in, g2, b2, h, a1, s1, n1, r1, s2, n2, r2):
    slot = base + pl.program_id(0)
    normed, inv = normalize(tok[0].astype(F32))
    n1[0] = normed.astype(BF16)
    r1[0] = spread(inv)
    act, slope = gelu_pair(normed * g1[...] + b1[...])
    act = act.astype(BF16)
    a1[0] = act
    s1[0] = slope.astype(BF16)
    hidden = dot(act, w_in[...]) + b_in[...]
    normed, inv = normalize(hidden)
    n2[0] = normed.astype(BF16)
    r2[0] = spread(inv)
    act, slope = gelu_pair(normed * g2[...] + b2[...])
    s2[0] = slope.astype(BF16)
    h[0] = jnp.where(keep_rows(win, slot, act.shape), act, 0.0).astype(BF16)


def rear_kernel(
    base, first, last, halves, rows, win, *refs
):
    pieces = refs[: 2 * halves + 1]
    refs = refs[2 * halves + 1 :]
    tok, cot, w_conv, b_conv, g3, b3, w_out, b_out = refs[:8]
    refs = refs[8:]
    if not first:
        wconv_in, wout_in, small_in = refs[:3]
        refs = refs[4:]
    out, dc_out, gw_conv, gw_out, small, acc_conv, acc_out, acc_small, strip = refs
    step = pl.program_id(0)

    @pl.when(step == 0)
    def _():
        if first:
            acc_conv[...] = jnp.zeros_like(acc_conv)
            acc_out[...] = jnp.zeros_like(acc_out)
            acc_small[...] = jnp.zeros_like(acc_small)
        else:
            acc_conv[...] = wconv_in[...]
            acc_out[...] = wout_in[...]
            acc_small[...] = small_in[...]

    slot = base + step
    at = 0
    for piece in pieces:
        count = piece.shape[1]
        strip[at : at + count] = piece[0]
        at += count
    inner = strip.shape[1]
    conv = dot(strip[0:rows], w_conv[0])
    for tap in range(1, TAPS):
        conv += dot(strip[tap * STEP : tap * STEP + rows], w_conv[tap])
    conv = (conv + b_conv[...]).astype(BF16).astype(F32)
    normed, inv = normalize(conv)
    act, slope = gelu_pair(normed * g3[...] + b3[...])
    act = act.astype(BF16)
    out[0] = (tok[0].astype(F32) + (dot(act, w_out[...]) + b_out[...])).astype(BF16)
    gy = jnp.where(keep_rows(win, slot, cot.shape[1:]), cot[0].astype(F32), 0.0)
    acc_small[0:1] += row_sum(gy)
    gy = gy.astype(BF16)
    acc_out[...] += dot_rows(act, gy)
    grad = dot_back(gy, w_out[...]) * slope
    acc_small[1:2, 0:inner] += row_sum(grad * normed)
    acc_small[1:2, inner : 2 * inner] += row_sum(grad)
    dc = norm_back(grad, normed, inv, g3[...]).astype(BF16)
    dc_out[0] = dc
    acc_small[2:3, 0:inner] += row_sum(dc.astype(F32))
    for tap in range(TAPS):
        acc_conv[tap] += dot_rows(strip[tap * STEP : tap * STEP + rows], dc)

    @pl.when(step == pl.num_programs(0) - 1)
    def _():
        kind = BF16 if last else F32
        gw_conv[...] = acc_conv[...].astype(kind)
        gw_out[...] = acc_out[...].astype(kind)
        small[...] = acc_small[...].astype(kind)


def back_kernel(base, first, last, halves, rows, win, *refs):
    pieces = refs[: 2 * halves + 1]
    refs = refs[2 * halves + 1 :]
    cot, a1, s1, n1, r1, s2, n2, r2, w_conv, g2, w_in, g1 = refs[:12]
    refs = refs[12:]
    if not first:
        win_in, small_in = refs[:2]
        refs = refs[3:]
    grad_out, gw_in, small, acc_in, acc_small, strip = refs
    step = pl.program_id(0)

    @pl.when(step == 0)
    def _():
        if first:
            acc_in[...] = jnp.zeros_like(acc_in)
            acc_small[...] = jnp.zeros_like(acc_small)
        else:
            acc_in[...] = win_in[...]
            acc_small[...] = small_in[...]

    slot = base + step
    at = 0
    for piece in pieces:
        count = piece.shape[1]
        strip[at : at + count] = piece[0]
        at += count
    inner = strip.shape[1]
    width = cot.shape[2]
    dh = dot_back(strip[2 * REACH : 2 * REACH + rows], w_conv[0])
    for tap in range(1, TAPS):
        begin = 2 * REACH - tap * STEP
        dh += dot_back(strip[begin : begin + rows], w_conv[tap])
    dh = jnp.where(keep_rows(win, slot, dh.shape), dh, 0.0).astype(BF16).astype(F32)
    grad = dh * s2[0].astype(F32)
    normed = n2[0].astype(F32)
    acc_small[2:3, 0:inner] += row_sum(grad * normed)
    acc_small[2:3, inner : 2 * inner] += row_sum(grad)
    inv = jnp.concatenate([r2[0]] * (inner // 128), axis=-1)
    dz = norm_back(grad, normed, inv, g2[...]).astype(BF16)
    acc_small[3:4, 0:inner] += row_sum(dz.astype(F32))
    acc_in[...] += dot_rows(a1[0], dz)
    grad = dot_back(dz, w_in[...]) * s1[0].astype(F32)
    normed = n1[0].astype(F32)
    acc_small[0:1] += row_sum(grad * normed)
    acc_small[1:2] += row_sum(grad)
    inv = jnp.concatenate([r1[0]] * (width // 128), axis=-1)
    branch = norm_back(grad, normed, inv, g1[...])
    gy = jnp.where(keep_rows(win, slot, cot.shape[1:]), cot[0].astype(F32), 0.0)
    grad_out[0] = (gy + branch).astype(BF16)

    @pl.when(step == pl.num_programs(0) - 1)
    def _():
        kind = BF16 if last else F32
        gw_in[...] = acc_in[...].astype(kind)
        small[...] = acc_small[...].astype(kind)


def whole(array):
    rank = array.ndim
    return pl.BlockSpec(array.shape, lambda i, w: (0,) * rank, pipeline_mode=pl.Buffered(1))


def per_slot(base, rows, width):
    return pl.BlockSpec((1, rows, width), lambda i, w: (base + i, 0, 0))


def call(kernel, win, args, specs, outs, out_specs, scratch, steps, flops, cost_bytes, aliases, name):
    return pl.pallas_call(
        kernel,
        out_shape=outs,
        grid_spec=pltpu.PrefetchScalarGridSpec(
            num_scalar_prefetch=1,
            grid=(steps,),
            in_specs=specs,
            out_specs=out_specs,
            scratch_shapes=scratch,
        ),
        compiler_params=pltpu.CompilerParams(
            dimension_semantics=("arbitrary",), vmem_limit_bytes=VMEM_LIMIT
        ),
        cost_estimate=pl.CostEstimate(
            flops=flops, bytes_accessed=cost_bytes, transcendentals=0
        ),
        input_output_aliases=aliases,
        name=name,
    )(win, *args)


def front(win, base, steps, tokens, g1, b1, w_in, b_in, g2, b2):
    _, rows, width = tokens.shape
    inner = w_in.shape[1]
    shape = lambda n, kind=BF16: jax.ShapeDtypeStruct((steps, rows, n), kind)
    outs = [shape(inner), shape(width), shape(width), shape(width), shape(128, F32)]
    outs += [shape(inner), shape(inner), shape(128, F32)]
    params = [g1, b1, w_in, b_in, g2, b2]
    return call(
        functools.partial(front_kernel, base),
        win,
        [tokens] + params,
        [per_slot(base, rows, width)] + [whole(p) for p in params],
        outs,
        [per_slot(0, rows, o.shape[2]) for o in outs],
        [],
        steps,
        6 * steps * rows * width * inner,
        steps * rows * width * 12,
        {},
        "front",
    )


def halo(values, hops, axis_size):
    before, after = [], []
    rows = values.shape[1]
    edge = min(rows, REACH)
    for hop in range(1, hops + 1):
        up = [(i, i + hop) for i in range(axis_size - hop)]
        down = [(i + hop, i) for i in range(axis_size - hop)]
        before.insert(0, lax.ppermute(values[:, rows - edge :], "seq", up))
        after.append(lax.ppermute(values[:, :edge], "seq", down))
    return before, after


def rear(win, base, steps, pieces, tokens, cot, params, carry, last):
    _, rows, width = tokens.shape
    w_conv, b_conv, g3, b3, w_out, b_out = params
    inner = w_conv.shape[2]
    halves = len(pieces) // 2
    first = carry is None
    args = list(pieces) + [tokens, cot] + params
    specs = [per_slot(0, p.shape[1], inner) for p in pieces]
    specs += [per_slot(base, rows, width)] * 2 + [whole(p) for p in params]
    aliases = {}
    if not first:
        args += carry[1:] + [carry[0]]
        specs += [whole(c) for c in carry[1:]] + [pl.BlockSpec(memory_space=pl.ANY)]
        aliases = {len(args): 0}
    kind = BF16 if last else F32
    outs = [
        jax.ShapeDtypeStruct(tokens.shape, BF16),
        jax.ShapeDtypeStruct((steps, rows, inner), BF16),
        jax.ShapeDtypeStruct(w_conv.shape, kind),
        jax.ShapeDtypeStruct(w_out.shape, kind),
        jax.ShapeDtypeStruct((8, width), kind),
    ]
    out_specs = [per_slot(base, rows, width), per_slot(0, rows, inner)]
    out_specs += [whole(o) for o in outs[2:]]
    scratch = [
        pltpu.VMEM(w_conv.shape, F32),
        pltpu.VMEM(w_out.shape, F32),
        pltpu.VMEM((8, width), F32),
        pltpu.VMEM((rows + 2 * REACH, inner), BF16),
    ]
    return call(
        functools.partial(rear_kernel, base, first, last, halves, rows),
        win,
        args,
        specs,
        outs,
        out_specs,
        scratch,
        steps,
        2 * steps * rows * inner * (2 * TAPS * inner + 3 * width),
        steps * rows * width * 10,
        aliases,
        "rear",
    )


def back(win, base, steps, pieces, cot, kept, params, carry, last):
    _, rows, width = cot.shape
    w_conv, g2, w_in, g1 = params
    inner = w_conv.shape[2]
    halves = len(pieces) // 2
    first = carry is None
    args = list(pieces) + [cot] + list(kept) + params
    specs = [per_slot(0, p.shape[1], inner) for p in pieces]
    specs += [per_slot(base, rows, width)]
    specs += [per_slot(0, rows, k.shape[2]) for k in kept] + [whole(p) for p in params]
    aliases = {}
    if not first:
        args += carry[1:] + [carry[0]]
        specs += [whole(c) for c in carry[1:]] + [pl.BlockSpec(memory_space=pl.ANY)]
        aliases = {len(args): 0}
    kind = BF16 if last else F32
    outs = [
        jax.ShapeDtypeStruct(cot.shape, BF16),
        jax.ShapeDtypeStruct(w_in.shape, kind),
        jax.ShapeDtypeStruct((8, width), kind),
    ]
    out_specs = [per_slot(base, rows, width)] + [whole(o) for o in outs[1:]]
    scratch = [
        pltpu.VMEM(w_in.shape, F32),
        pltpu.VMEM((8, width), F32),
        pltpu.VMEM((rows + 2 * REACH, inner), BF16),
    ]
    return call(
        functools.partial(back_kernel, base, first, last, halves, rows),
        win,
        args,
        specs,
        outs,
        out_specs,
        scratch,
        steps,
        2 * steps * rows * inner * (TAPS * inner + 2 * width),
        steps * rows * width * 12,
        aliases,
        "back",
    )


def body(
    tokens,
    cotangent,
    ln1_gain,
    ln1_bias,
    w_in,
    b_in,
    ln2_gain,
    ln2_bias,
    w_conv,
    b_conv,
    ln3_gain,
    ln3_bias,
    w_out,
    b_out,
    lengths,
    offsets,
    live,
):
    axis_size = lax.axis_size("seq")
    slots, rows, width = tokens.shape
    inner = w_in.shape[1]
    hops = -(-REACH // rows)
    begin = lax.axis_index("seq") * rows
    filled = jnp.arange(slots, dtype=jnp.int32) < live[0]
    low = jnp.clip(offsets - begin, 0, rows)
    high = jnp.where(filled, jnp.clip(offsets + lengths - begin, 0, rows), 0)
    win = jnp.stack([low, high])
    flat = lambda v: v.astype(F32).reshape(1, -1)
    g1, b1, g2, b2, g3, b3 = map(
        flat, (ln1_gain, ln1_bias, ln2_gain, ln2_bias, ln3_gain, ln3_bias)
    )
    chunks = 2
    steps = slots // chunks
    fronts = [
        front(win, c * steps, steps, tokens, g1, b1, w_in, flat(b_in), g2, b2)
        for c in range(chunks)
    ]
    carry = None
    grads = []
    params = [w_conv, flat(b_conv), g3, b3, w_out, flat(b_out)]
    for c in range(chunks):
        before, after = halo(fronts[c][0], hops, axis_size)
        pieces = before + [fronts[c][0]] + after
        res = rear(
            win, c * steps, steps, pieces, tokens, cotangent, params, carry, c == chunks - 1
        )
        grads.append(res[1])
        carry = [res[0]] + list(res[2:])
    output = carry[0]
    gw_conv, gw_out, small_rear = lax.psum(tuple(carry[1:]), ("dp", "seq"))
    carry = None
    params = [w_conv, g2, w_in, g1]
    for c in range(chunks):
        before, after = halo(grads[c], hops, axis_size)
        pieces = before + [grads[c]] + after
        res = back(
            win, c * steps, steps, pieces, cotangent, fronts[c][1:], params, carry, c == chunks - 1
        )
        carry = list(res)
    grad_tokens = carry[0]
    gw_conv, gw_out, small_rear, late = lax.optimization_barrier(
        (gw_conv, gw_out, small_rear, tuple(carry[1:]))
    )
    gw_in, small_back = lax.psum(late, ("dp", "seq"))
    small_rear = small_rear.astype(F32)
    small_back = small_back.astype(F32)
    return (
        output,
        grad_tokens,
        small_back[0],
        small_back[1],
        gw_in.astype(F32),
        small_back[3, :inner],
        small_back[2, :inner],
        small_back[2, inner : 2 * inner],
        gw_conv.astype(F32),
        small_rear[2, :inner],
        small_rear[1, :inner],
        small_rear[1, inner : 2 * inner],
        gw_out.astype(F32),
        small_rear[0],
    )


def solution(mesh):
    return jax.shard_map(
        body,
        mesh=mesh,
        in_specs=(P("dp", "seq", None),) * 2 + (P(),) * 12 + (P("dp"),) * 3,
        out_specs=(P("dp", "seq", None),) * 2 + (P(),) * 12,
        check_vma=False,
    )
```

```python
import functools

import jax
import jax.numpy as jnp
from jax import lax
from jax.experimental import pallas as pl
from jax.experimental.pallas import tpu as pltpu
from jax.sharding import PartitionSpec as P

TAPS = 5
STEP = 128
REACH = (TAPS - 1) // 2 * STEP
EPSILON = 1e-05
SQRT_HALF = 0.7071067811865476
INV_ROOT_TAU = 0.3989422804014327
G1, B1, BIN, G2, B2, BCONV, G3, B3, BOUT = range(9)
VMEM_LIMIT = 60 * 1024 * 1024
F32 = jnp.float32
BF16 = jnp.bfloat16


def dot(left, right):
    return jnp.dot(left, right, preferred_element_type=F32)


def dot_back(left, right):
    return lax.dot_general(left, right, (((1,), (1,)), ((), ())), preferred_element_type=F32)


def dot_rows(left, right):
    return lax.dot_general(left, right, (((0,), (0,)), ((), ())), preferred_element_type=F32)


def normalize(values):
    centre = values - jnp.mean(values, axis=-1, keepdims=True)
    inv = lax.rsqrt(jnp.mean(centre * centre, axis=-1, keepdims=True) + EPSILON)
    return centre * inv, inv


def gelu_pair(values):
    gate = 0.5 + 0.5 * lax.erf(values * SQRT_HALF)
    slope = gate + values * (INV_ROOT_TAU * jnp.exp(-0.5 * values * values))
    return values * gate, slope


def norm_back(grad, normed, inv, gain):
    scaled = grad * gain
    return inv * (
        scaled
        - jnp.mean(scaled, axis=-1, keepdims=True)
        - normed * jnp.mean(scaled * normed, axis=-1, keepdims=True)
    )


def keep_rows(win_ref, slot, shape):
    rows = lax.broadcasted_iota(jnp.int32, shape, 0)
    return (rows >= win_ref[0, slot]) & (rows < win_ref[1, slot])


def row_sum(values):
    return jnp.sum(values, axis=0, keepdims=True)


def spread(inv):
    return jnp.broadcast_to(inv, (inv.shape[0], 128))


def front_kernel(base, win, tok, w_in, table, h, a1, s1, n1, r1, s2, n2, r2):
    slot = base + pl.program_id(0)
    inner = w_in.shape[1]
    g1, b1 = table[G1 : G1 + 1], table[B1 : B1 + 1]
    g2, b2 = table[G2 : G2 + 1, :inner], table[B2 : B2 + 1, :inner]
    b_in = table[BIN : BIN + 1, :inner]
    normed, inv = normalize(tok[0].astype(F32))
    n1[0] = normed.astype(BF16)
    r1[0] = spread(inv)
    act, slope = gelu_pair(normed * g1 + b1)
    act = act.astype(BF16)
    a1[0] = act
    s1[0] = slope.astype(BF16)
    hidden = dot(act, w_in[...]) + b_in
    normed, inv = normalize(hidden)
    n2[0] = normed.astype(BF16)
    r2[0] = spread(inv)
    act, slope = gelu_pair(normed * g2 + b2)
    s2[0] = slope.astype(BF16)
    h[0] = jnp.where(keep_rows(win, slot, act.shape), act, 0.0).astype(BF16)


def rear_kernel(
    base, first, last, halves, rows, win, *refs
):
    pieces = refs[: 2 * halves + 1]
    refs = refs[2 * halves + 1 :]
    tok, cot, w_conv, w_out, table = refs[:5]
    refs = refs[5:]
    if not first:
        wconv_in, wout_in, small_in = refs[:3]
        refs = refs[4:]
    out, dc_out, gw_conv, gw_out, small, acc_conv, acc_out, acc_small, strip = refs
    step = pl.program_id(0)

    @pl.when(step == 0)
    def _():
        if first:
            acc_conv[...] = jnp.zeros_like(acc_conv)
            acc_out[...] = jnp.zeros_like(acc_out)
            acc_small[...] = jnp.zeros_like(acc_small)
        else:
            acc_conv[...] = wconv_in[...]
            acc_out[...] = wout_in[...]
            acc_small[...] = small_in[...]

    slot = base + step
    at = 0
    for piece in pieces:
        count = piece.shape[1]
        strip[at : at + count] = piece[0]
        at += count
    inner = strip.shape[1]
    g3, b3 = table[G3 : G3 + 1, :inner], table[B3 : B3 + 1, :inner]
    b_conv, b_out = table[BCONV : BCONV + 1, :inner], table[BOUT : BOUT + 1]
    conv = dot(strip[0:rows], w_conv[0])
    for tap in range(1, TAPS):
        conv += dot(strip[tap * STEP : tap * STEP + rows], w_conv[tap])
    conv = (conv + b_conv).astype(BF16).astype(F32)
    normed, inv = normalize(conv)
    act, slope = gelu_pair(normed * g3 + b3)
    act = act.astype(BF16)
    out[0] = (tok[0].astype(F32) + (dot(act, w_out[...]) + b_out)).astype(BF16)
    gy = jnp.where(keep_rows(win, slot, cot.shape[1:]), cot[0].astype(F32), 0.0)
    acc_small[0:1] += row_sum(gy)
    gy = gy.astype(BF16)
    acc_out[...] += dot_rows(act, gy)
    grad = dot_back(gy, w_out[...]) * slope
    acc_small[1:2, 0:inner] += row_sum(grad * normed)
    acc_small[1:2, inner : 2 * inner] += row_sum(grad)
    dc = norm_back(grad, normed, inv, g3).astype(BF16)
    dc_out[0] = dc
    acc_small[2:3, 0:inner] += row_sum(dc.astype(F32))
    for tap in range(TAPS):
        acc_conv[tap] += dot_rows(strip[tap * STEP : tap * STEP + rows], dc)

    @pl.when(step == pl.num_programs(0) - 1)
    def _():
        kind = BF16 if last else F32
        gw_conv[...] = acc_conv[...].astype(kind)
        gw_out[...] = acc_out[...].astype(kind)
        small[...] = acc_small[...]


def back_kernel(base, first, last, halves, rows, win, *refs):
    pieces = refs[: 2 * halves + 1]
    refs = refs[2 * halves + 1 :]
    cot, a1, s1, n1, r1, s2, n2, r2, w_conv, w_in, table = refs[:11]
    refs = refs[11:]
    if not first:
        win_in, small_in = refs[:2]
        refs = refs[3:]
    grad_out, gw_in, small, acc_in, acc_small, strip = refs
    step = pl.program_id(0)

    @pl.when(step == 0)
    def _():
        if first:
            acc_in[...] = jnp.zeros_like(acc_in)
            acc_small[...] = jnp.zeros_like(acc_small)
        else:
            acc_in[...] = win_in[...]
            acc_small[...] = small_in[...]

    slot = base + step
    at = 0
    for piece in pieces:
        count = piece.shape[1]
        strip[at : at + count] = piece[0]
        at += count
    inner = strip.shape[1]
    g1, g2 = table[G1 : G1 + 1], table[G2 : G2 + 1, :inner]
    width = cot.shape[2]
    dh = dot_back(strip[2 * REACH : 2 * REACH + rows], w_conv[0])
    for tap in range(1, TAPS):
        begin = 2 * REACH - tap * STEP
        dh += dot_back(strip[begin : begin + rows], w_conv[tap])
    dh = jnp.where(keep_rows(win, slot, dh.shape), dh, 0.0).astype(BF16).astype(F32)
    grad = dh * s2[0].astype(F32)
    normed = n2[0].astype(F32)
    acc_small[2:3, 0:inner] += row_sum(grad * normed)
    acc_small[2:3, inner : 2 * inner] += row_sum(grad)
    inv = jnp.concatenate([r2[0]] * (inner // 128), axis=-1)
    dz = norm_back(grad, normed, inv, g2).astype(BF16)
    acc_small[3:4, 0:inner] += row_sum(dz.astype(F32))
    acc_in[...] += dot_rows(a1[0], dz)
    grad = dot_back(dz, w_in[...]) * s1[0].astype(F32)
    normed = n1[0].astype(F32)
    acc_small[0:1] += row_sum(grad * normed)
    acc_small[1:2] += row_sum(grad)
    inv = jnp.concatenate([r1[0]] * (width // 128), axis=-1)
    branch = norm_back(grad, normed, inv, g1)
    gy = jnp.where(keep_rows(win, slot, cot.shape[1:]), cot[0].astype(F32), 0.0)
    grad_out[0] = (gy + branch).astype(BF16)

    @pl.when(step == pl.num_programs(0) - 1)
    def _():
        if last:
            depth = acc_in.shape[0] // 16
            for col in range(inner // 128):
                part = acc_in[:, col * 128 : (col + 1) * 128].reshape(depth, 16, 128)
                gw_in[col * depth : (col + 1) * depth] = part.astype(BF16)
        else:
            gw_in[...] = acc_in[...]
        small[...] = acc_small[...]


def whole(array):
    rank = array.ndim
    return pl.BlockSpec(array.shape, lambda i, w: (0,) * rank, pipeline_mode=pl.Buffered(1))


def per_slot(base, rows, width):
    return pl.BlockSpec((1, rows, width), lambda i, w: (base + i, 0, 0))


def call(kernel, win, args, specs, outs, out_specs, scratch, steps, flops, cost_bytes, aliases, name):
    return pl.pallas_call(
        kernel,
        out_shape=outs,
        grid_spec=pltpu.PrefetchScalarGridSpec(
            num_scalar_prefetch=1,
            grid=(steps,),
            in_specs=specs,
            out_specs=out_specs,
            scratch_shapes=scratch,
        ),
        compiler_params=pltpu.CompilerParams(
            dimension_semantics=("arbitrary",), vmem_limit_bytes=VMEM_LIMIT
        ),
        cost_estimate=pl.CostEstimate(
            flops=flops, bytes_accessed=cost_bytes, transcendentals=0
        ),
        input_output_aliases=aliases,
        name=name,
    )(win, *args)


def front(win, base, steps, tokens, w_in, table):
    _, rows, width = tokens.shape
    inner = w_in.shape[1]
    shape = lambda n, kind=BF16: jax.ShapeDtypeStruct((steps, rows, n), kind)
    outs = [shape(inner), shape(width), shape(width), shape(width), shape(128, F32)]
    outs += [shape(inner), shape(inner), shape(128, F32)]
    params = [w_in, table]
    return call(
        functools.partial(front_kernel, base),
        win,
        [tokens] + params,
        [per_slot(base, rows, width)] + [whole(p) for p in params],
        outs,
        [per_slot(0, rows, o.shape[2]) for o in outs],
        [],
        steps,
        6 * steps * rows * width * inner,
        steps * rows * width * 12,
        {},
        "front",
    )


def halo(values, hops, axis_size):
    before, after = [], []
    rows = values.shape[1]
    edge = min(rows, REACH)
    for hop in range(1, hops + 1):
        up = [(i, i + hop) for i in range(axis_size - hop)]
        down = [(i + hop, i) for i in range(axis_size - hop)]
        before.insert(0, lax.ppermute(values[:, rows - edge :], "seq", up))
        after.append(lax.ppermute(values[:, :edge], "seq", down))
    return before, after


def rear(win, base, steps, pieces, tokens, cot, params, carry, last):
    _, rows, width = tokens.shape
    w_conv, w_out, _ = params
    inner = w_conv.shape[2]
    halves = len(pieces) // 2
    first = carry is None
    args = list(pieces) + [tokens, cot] + params
    specs = [per_slot(0, p.shape[1], inner) for p in pieces]
    specs += [per_slot(base, rows, width)] * 2 + [whole(p) for p in params]
    aliases = {}
    if not first:
        args += carry[1:] + [carry[0]]
        specs += [whole(c) for c in carry[1:]] + [pl.BlockSpec(memory_space=pl.ANY)]
        aliases = {len(args): 0}
    kind = BF16 if last else F32
    outs = [
        jax.ShapeDtypeStruct(tokens.shape, BF16),
        jax.ShapeDtypeStruct((steps, rows, inner), BF16),
        jax.ShapeDtypeStruct(w_conv.shape, kind),
        jax.ShapeDtypeStruct(w_out.shape, kind),
        jax.ShapeDtypeStruct((8, width), F32),
    ]
    out_specs = [per_slot(base, rows, width), per_slot(0, rows, inner)]
    out_specs += [whole(o) for o in outs[2:]]
    scratch = [
        pltpu.VMEM(w_conv.shape, F32),
        pltpu.VMEM(w_out.shape, F32),
        pltpu.VMEM((8, width), F32),
        pltpu.VMEM((rows + 2 * REACH, inner), BF16),
    ]
    return call(
        functools.partial(rear_kernel, base, first, last, halves, rows),
        win,
        args,
        specs,
        outs,
        out_specs,
        scratch,
        steps,
        2 * steps * rows * inner * (2 * TAPS * inner + 3 * width),
        steps * rows * width * 10,
        aliases,
        "rear",
    )


def back(win, base, steps, pieces, cot, kept, params, carry, last):
    _, rows, width = cot.shape
    w_conv, w_in, _ = params
    inner = w_conv.shape[2]
    halves = len(pieces) // 2
    first = carry is None
    args = list(pieces) + [cot] + list(kept) + params
    specs = [per_slot(0, p.shape[1], inner) for p in pieces]
    specs += [per_slot(base, rows, width)]
    specs += [per_slot(0, rows, k.shape[2]) for k in kept] + [whole(p) for p in params]
    aliases = {}
    if not first:
        args += carry[1:] + [carry[0]]
        specs += [whole(c) for c in carry[1:]] + [pl.BlockSpec(memory_space=pl.ANY)]
        aliases = {len(args): 0}
    kind = BF16 if last else F32
    outs = [
        jax.ShapeDtypeStruct(cot.shape, BF16),
        jax.ShapeDtypeStruct((w_in.size // 2048, 16, 128) if last else w_in.shape, kind),
        jax.ShapeDtypeStruct((8, width), F32),
    ]
    out_specs = [per_slot(base, rows, width)] + [whole(o) for o in outs[1:]]
    scratch = [
        pltpu.VMEM(w_in.shape, F32),
        pltpu.VMEM((8, width), F32),
        pltpu.VMEM((rows + 2 * REACH, inner), BF16),
    ]
    return call(
        functools.partial(back_kernel, base, first, last, halves, rows),
        win,
        args,
        specs,
        outs,
        out_specs,
        scratch,
        steps,
        2 * steps * rows * inner * (TAPS * inner + 2 * width),
        steps * rows * width * 12,
        aliases,
        "back",
    )


def sum_kernel(grid_shape, tiles, gw, small_a, small_b, out, small, mine, got, half, got_x, part, got_d, full, sends, recvs):
    d_size, x_size = grid_shape
    seq, dp = lax.axis_index("seq"), lax.axis_index("dp")
    core, x = lax.rem(seq, 2), lax.div(seq, 2)
    sibling = {"seq": seq + 1 - 2 * core}
    x_peers = [{"seq": 2 * lax.rem(x + o, x_size) + core} for o in range(1, x_size)]
    d_peers = [{"dp": lax.rem(dp + o, d_size)} for o in range(1, d_size)]
    peers = [sibling] + x_peers + d_peers
    barrier = pltpu.get_barrier_semaphore()
    for peer in peers:
        pl.semaphore_signal(barrier, inc=1, device_id=peer, device_id_type=pl.DeviceIdType.MESH)
    used = gw.shape[0]
    mine[0:used] = gw[...]
    columns = small_a.shape[1] // 128
    for col in range(columns):
        lanes = slice(col * 128, (col + 1) * 128)
        mine[used + col] = jnp.concatenate([small_a[:, lanes], small_b[:, lanes]], axis=0).astype(
            BF16
        )
    spare = mine.shape[0] - used - columns
    if spare:
        mine[used + columns :] = jnp.zeros((spare, 16, 128), BF16)
    pl.semaphore_wait(barrier, len(peers))
    count = [0]

    def send(src, dst, peer):
        at = count[0]
        count[0] += 1
        copy = pltpu.make_async_remote_copy(
            src_ref=src,
            dst_ref=dst,
            send_sem=sends.at[at],
            recv_sem=recvs.at[at],
            device_id=peer,
            device_id_type=pl.DeviceIdType.MESH,
        )
        copy.start()
        return copy

    x_tiles = d_size * tiles
    core_tiles = x_size * x_tiles
    copies = [send(mine.at[pl.ds((1 - core) * core_tiles, core_tiles)], got, sibling)]
    copies[0].wait_recv()
    half[...] = (
        mine[pl.ds(core * core_tiles, core_tiles)].astype(F32) + got[...].astype(F32)
    ).astype(BF16)
    now = []
    for o, peer in enumerate(x_peers):
        target = lax.rem(x + o + 1, x_size)
        now.append(send(half.at[pl.ds(target * x_tiles, x_tiles)], got_x.at[o], peer))
    for copy in now:
        copy.wait_recv()
    copies += now
    total = half[pl.ds(x * x_tiles, x_tiles)].astype(F32)
    for o in range(x_size - 1):
        total += got_x[o].astype(F32)
    part[...] = total.astype(BF16)
    now = []
    for o, peer in enumerate(d_peers):
        target = lax.rem(dp + o + 1, d_size)
        now.append(send(part.at[pl.ds(target * tiles, tiles)], got_d.at[o], peer))
    for copy in now:
        copy.wait_recv()
    copies += now
    total = part[pl.ds(dp * tiles, tiles)].astype(F32)
    for o in range(d_size - 1):
        total += got_d[o].astype(F32)
    home_x = core * core_tiles + x * x_tiles
    own = pl.ds(home_x + dp * tiles, tiles)
    full[own] = total.astype(BF16)
    for peers, span in (
        (d_peers, own),
        (x_peers, pl.ds(home_x, x_tiles)),
        ([sibling], pl.ds(core * core_tiles, core_tiles)),
    ):
        now = [send(full.at[span], full.at[span], peer) for peer in peers]
        for copy in now:
            copy.wait_recv()
        copies += now
    for copy in copies:
        copy.wait_send()
    depth = out.shape[0] // 16
    for col in range(out.shape[1] // 128):
        piece = full[col * depth : (col + 1) * depth].astype(F32)
        out[:, col * 128 : (col + 1) * 128] = piece.reshape(out.shape[0], 128)
    for col in range(columns):
        small[:, col * 128 : (col + 1) * 128] = full[used + col].astype(F32)


def sum_all(gw, small_a, small_b, shape):
    d_size, x_size = lax.axis_size("dp"), lax.axis_size("seq") // 2
    devices = 2 * d_size * x_size
    tiles = -(-(gw.shape[0] + small_a.shape[1] // 128) // devices)
    x_tiles = d_size * tiles
    copies = 2 * (1 + x_size - 1 + d_size - 1)
    block = lambda *lead: pltpu.VMEM((*lead, 16, 128), BF16)
    return pl.pallas_call(
        functools.partial(sum_kernel, (d_size, x_size), tiles),
        out_shape=[
            jax.ShapeDtypeStruct(shape, F32),
            jax.ShapeDtypeStruct((16, small_a.shape[1]), F32),
        ],
        in_specs=[pl.BlockSpec(memory_space=pltpu.VMEM)] * 3,
        out_specs=[pl.BlockSpec(memory_space=pltpu.VMEM)] * 2,
        scratch_shapes=[
            block(devices * tiles),
            block(x_size * x_tiles),
            block(x_size * x_tiles),
            block(x_size - 1, x_tiles),
            block(x_tiles),
            block(d_size - 1, tiles),
            block(devices * tiles),
            pltpu.SemaphoreType.DMA((copies,)),
            pltpu.SemaphoreType.DMA((copies,)),
        ],
        compiler_params=pltpu.CompilerParams(collective_id=0, has_side_effects=True),
        cost_estimate=pl.CostEstimate(flops=0, bytes_accessed=120_000_000, transcendentals=0),
        name="sum_all",
    )(gw, small_a, small_b)


def body(
    tokens,
    cotangent,
    ln1_gain,
    ln1_bias,
    w_in,
    b_in,
    ln2_gain,
    ln2_bias,
    w_conv,
    b_conv,
    ln3_gain,
    ln3_bias,
    w_out,
    b_out,
    lengths,
    offsets,
    live,
):
    axis_size = lax.axis_size("seq")
    slots, rows, width = tokens.shape
    inner = w_in.shape[1]
    hops = -(-REACH // rows)
    begin = lax.axis_index("seq") * rows
    filled = jnp.arange(slots, dtype=jnp.int32) < live[0]
    low = jnp.clip(offsets - begin, 0, rows)
    high = jnp.where(filled, jnp.clip(offsets + lengths - begin, 0, rows), 0)
    win = jnp.stack([low, high])
    table = jnp.stack(
        [
            jnp.pad(v.astype(F32), (0, width - v.shape[0]))
            for v in (ln1_gain, ln1_bias, b_in, ln2_gain, ln2_bias, b_conv, ln3_gain, ln3_bias, b_out)
        ]
    )
    chunks = 2
    steps = slots // chunks
    fronts = [
        front(win, c * steps, steps, tokens, w_in, table)
        for c in range(chunks)
    ]
    carry = None
    grads = []
    params = [w_conv, w_out, table]
    for c in range(chunks):
        before, after = halo(fronts[c][0], hops, axis_size)
        pieces = before + [fronts[c][0]] + after
        res = rear(
            win, c * steps, steps, pieces, tokens, cotangent, params, carry, c == chunks - 1
        )
        grads.append(res[1])
        carry = [res[0]] + list(res[2:])
    output = carry[0]
    gw_conv, gw_out = lax.psum(tuple(carry[1:3]), ("dp", "seq"))
    small_rear = carry[3]
    carry = None
    params = [w_conv, w_in, table]
    for c in range(chunks):
        before, after = halo(grads[c], hops, axis_size)
        pieces = before + [grads[c]] + after
        res = back(
            win, c * steps, steps, pieces, cotangent, fronts[c][1:], params, carry, c == chunks - 1
        )
        carry = list(res)
    grad_tokens = carry[0]
    gw_in, smalls = sum_all(carry[1], small_rear, carry[2], w_in.shape)
    small_rear, small_back = smalls[:8], smalls[8:]
    return (
        output,
        grad_tokens,
        small_back[0],
        small_back[1],
        gw_in,
        small_back[3, :inner],
        small_back[2, :inner],
        small_back[2, inner : 2 * inner],
        gw_conv.astype(F32),
        small_rear[2, :inner],
        small_rear[1, :inner],
        small_rear[1, inner : 2 * inner],
        gw_out.astype(F32),
        small_rear[0],
    )


def solution(mesh):
    return jax.shard_map(
        body,
        mesh=mesh,
        in_specs=(P("dp", "seq", None),) * 2 + (P(),) * 12 + (P("dp"),) * 3,
        out_specs=(P("dp", "seq", None),) * 2 + (P(),) * 12,
        check_vma=False,
    )
```

```python
import functools

import jax
import jax.numpy as jnp
from jax import lax
from jax.experimental import pallas as pl
from jax.experimental.pallas import tpu as pltpu
from jax.sharding import PartitionSpec as P

TAPS = 5
STEP = 128
REACH = (TAPS - 1) // 2 * STEP
EPSILON = 1e-05
SQRT_HALF = 0.7071067811865476
INV_ROOT_TAU = 0.3989422804014327
G1, B1, BIN, G2, B2, BCONV, G3, B3, BOUT = range(9)
VMEM_LIMIT = 60 * 1024 * 1024
F32 = jnp.float32
BF16 = jnp.bfloat16


def dot(left, right):
    return jnp.dot(left, right, preferred_element_type=F32)


def dot_back(left, right):
    return lax.dot_general(left, right, (((1,), (1,)), ((), ())), preferred_element_type=F32)


def dot_rows(left, right):
    return lax.dot_general(left, right, (((0,), (0,)), ((), ())), preferred_element_type=F32)


def normalize(values):
    centre = values - jnp.mean(values, axis=-1, keepdims=True)
    inv = lax.rsqrt(jnp.mean(centre * centre, axis=-1, keepdims=True) + EPSILON)
    return centre * inv, inv


def gelu_pair(values):
    gate = 0.5 + 0.5 * lax.erf(values * SQRT_HALF)
    slope = gate + values * (INV_ROOT_TAU * jnp.exp(-0.5 * values * values))
    return values * gate, slope


def norm_back(grad, normed, inv, gain):
    scaled = grad * gain
    return inv * (
        scaled
        - jnp.mean(scaled, axis=-1, keepdims=True)
        - normed * jnp.mean(scaled * normed, axis=-1, keepdims=True)
    )


def keep_rows(win_ref, slot, shape):
    rows = lax.broadcasted_iota(jnp.int32, shape, 0)
    return (rows >= win_ref[0, slot]) & (rows < win_ref[1, slot])


def row_sum(values):
    return jnp.sum(values, axis=0, keepdims=True)


def spread(inv):
    return jnp.broadcast_to(inv, (inv.shape[0], 128))


def front_kernel(base, win, tok, w_in, table, h, a1, s1, n1, r1, s2, n2, r2):
    slot = base + pl.program_id(0)
    inner = w_in.shape[1]
    g1, b1 = table[G1 : G1 + 1], table[B1 : B1 + 1]
    g2, b2 = table[G2 : G2 + 1, :inner], table[B2 : B2 + 1, :inner]
    b_in = table[BIN : BIN + 1, :inner]
    active = win[1, slot] > win[0, slot]

    @pl.when(active)
    def _():
        normed, inv = normalize(tok[0].astype(F32))
        n1[0] = normed.astype(BF16)
        r1[0] = spread(inv)
        act, slope = gelu_pair(normed * g1 + b1)
        act = act.astype(BF16)
        a1[0] = act
        s1[0] = slope.astype(BF16)
        hidden = dot(act, w_in[...]) + b_in
        normed, inv = normalize(hidden)
        n2[0] = normed.astype(BF16)
        r2[0] = spread(inv)
        act, slope = gelu_pair(normed * g2 + b2)
        s2[0] = slope.astype(BF16)
        h[0] = jnp.where(keep_rows(win, slot, act.shape), act, 0.0).astype(BF16)

    @pl.when(jnp.logical_not(active))
    def _():
        h[0] = jnp.zeros(h.shape[1:], BF16)


def rear_kernel(
    base, first, last, halves, rows, win, *refs
):
    pieces = refs[: 2 * halves + 1]
    refs = refs[2 * halves + 1 :]
    cot, w_conv, w_out, table = refs[:4]
    refs = refs[4:]
    if not first:
        wconv_in, wout_in, small_in = refs[:3]
        refs = refs[3:]
    a3, dc_out, gw_conv, gw_out, small, acc_conv, acc_out, acc_small, strip = refs
    step = pl.program_id(0)

    @pl.when(step == 0)
    def _():
        if first:
            acc_conv[...] = jnp.zeros_like(acc_conv)
            acc_out[...] = jnp.zeros_like(acc_out)
            acc_small[...] = jnp.zeros_like(acc_small)
        else:
            acc_conv[...] = wconv_in[...]
            acc_out[...] = wout_in[...]
            acc_small[...] = small_in[...]

    slot = base + step
    at = 0
    for piece in pieces:
        count = piece.shape[1]
        strip[at : at + count] = piece[0]
        at += count
    inner = strip.shape[1]
    g3, b3 = table[G3 : G3 + 1, :inner], table[B3 : B3 + 1, :inner]
    b_conv = table[BCONV : BCONV + 1, :inner]

    conv = dot(strip[0:rows], w_conv[0])
    for tap in range(1, TAPS):
        conv += dot(strip[tap * STEP : tap * STEP + rows], w_conv[tap])
    conv = (conv + b_conv).astype(BF16).astype(F32)
    normed, inv = normalize(conv)
    act, slope = gelu_pair(normed * g3 + b3)
    act = act.astype(BF16)
    a3[0] = act
    active = win[1, slot] > win[0, slot]

    @pl.when(active)
    def _():
        gy = jnp.where(keep_rows(win, slot, cot.shape[1:]), cot[0].astype(F32), 0.0)
        acc_small[0:1] += row_sum(gy)
        gy = gy.astype(BF16)
        acc_out[...] += dot_rows(act, gy)
        grad = dot_back(gy, w_out[...]) * slope
        acc_small[1:2, 0:inner] += row_sum(grad * normed)
        acc_small[1:2, inner : 2 * inner] += row_sum(grad)
        dc = norm_back(grad, normed, inv, g3).astype(BF16)
        dc_out[0] = dc
        acc_small[2:3, 0:inner] += row_sum(dc.astype(F32))
        for tap in range(TAPS):
            acc_conv[tap] += dot_rows(strip[tap * STEP : tap * STEP + rows], dc)

    @pl.when(jnp.logical_not(active))
    def _():
        dc_out[0] = jnp.zeros(dc_out.shape[1:], BF16)

    @pl.when(step == pl.num_programs(0) - 1)
    def _():
        kind = BF16 if last else F32
        gw_conv[...] = acc_conv[...].astype(kind)
        gw_out[...] = acc_out[...].astype(kind)
        small[...] = acc_small[...]


def back_kernel(base, first, last, halves, rows, win, *refs):
    pieces = refs[: 2 * halves + 1]
    refs = refs[2 * halves + 1 :]
    tok, cot, a1, s1, n1, r1, s2, n2, r2, a3, w_conv, w_in, w_out, table = refs[:14]
    refs = refs[14:]
    if not first:
        win_in, small_in = refs[:2]
        refs = refs[4:]
    out, grad_out, gw_in, small, acc_in, acc_small, strip = refs
    step = pl.program_id(0)

    @pl.when(step == 0)
    def _():
        if first:
            acc_in[...] = jnp.zeros_like(acc_in)
            acc_small[...] = jnp.zeros_like(acc_small)
        else:
            acc_in[...] = win_in[...]
            acc_small[...] = small_in[...]

    slot = base + step
    at = 0
    for piece in pieces:
        count = piece.shape[1]
        strip[at : at + count] = piece[0]
        at += count
    inner = strip.shape[1]
    g1, g2 = table[G1 : G1 + 1], table[G2 : G2 + 1, :inner]
    width = cot.shape[2]

    def residual():
        sent = dot(a3[0], w_out[...]) + table[BOUT : BOUT + 1]
        out[0] = (tok[0].astype(F32) + sent).astype(BF16)

    active = win[1, slot] > win[0, slot]

    @pl.when(active)
    def _():
        residual()
        dh = dot_back(strip[2 * REACH : 2 * REACH + rows], w_conv[0])
        for tap in range(1, TAPS):
            begin = 2 * REACH - tap * STEP
            dh += dot_back(strip[begin : begin + rows], w_conv[tap])
        dh = jnp.where(keep_rows(win, slot, dh.shape), dh, 0.0).astype(BF16).astype(F32)
        grad = dh * s2[0].astype(F32)
        normed = n2[0].astype(F32)
        acc_small[2:3, 0:inner] += row_sum(grad * normed)
        acc_small[2:3, inner : 2 * inner] += row_sum(grad)
        inv = jnp.concatenate([r2[0]] * (inner // 128), axis=-1)
        dz = norm_back(grad, normed, inv, g2).astype(BF16)
        acc_small[3:4, 0:inner] += row_sum(dz.astype(F32))
        acc_in[...] += dot_rows(a1[0], dz)
        grad = dot_back(dz, w_in[...]) * s1[0].astype(F32)
        normed = n1[0].astype(F32)
        acc_small[0:1] += row_sum(grad * normed)
        acc_small[1:2] += row_sum(grad)
        inv = jnp.concatenate([r1[0]] * (width // 128), axis=-1)
        branch = norm_back(grad, normed, inv, g1)
        gy = jnp.where(keep_rows(win, slot, cot.shape[1:]), cot[0].astype(F32), 0.0)
        grad_out[0] = (gy + branch).astype(BF16)

    @pl.when(jnp.logical_not(active))
    def _():
        residual()
        grad_out[0] = jnp.zeros(grad_out.shape[1:], BF16)

    @pl.when(step == pl.num_programs(0) - 1)
    def _():
        if last:
            depth = acc_in.shape[0] // 16
            for col in range(inner // 128):
                part = acc_in[:, col * 128 : (col + 1) * 128].reshape(depth, 16, 128)
                gw_in[col * depth : (col + 1) * depth] = part.astype(BF16)
        else:
            gw_in[...] = acc_in[...]
        small[...] = acc_small[...]


def whole(array):
    rank = array.ndim
    return pl.BlockSpec(array.shape, lambda i, w: (0,) * rank, pipeline_mode=pl.Buffered(1))


def per_slot(base, rows, width):
    return pl.BlockSpec((1, rows, width), lambda i, w: (base + i, 0, 0))


def call(kernel, win, args, specs, outs, out_specs, scratch, steps, flops, cost_bytes, aliases, name):
    return pl.pallas_call(
        kernel,
        out_shape=outs,
        grid_spec=pltpu.PrefetchScalarGridSpec(
            num_scalar_prefetch=1,
            grid=(steps,),
            in_specs=specs,
            out_specs=out_specs,
            scratch_shapes=scratch,
        ),
        compiler_params=pltpu.CompilerParams(
            dimension_semantics=("arbitrary",), vmem_limit_bytes=VMEM_LIMIT
        ),
        cost_estimate=pl.CostEstimate(
            flops=flops, bytes_accessed=cost_bytes, transcendentals=0
        ),
        input_output_aliases=aliases,
        name=name,
    )(win, *args)


def front(win, base, steps, tokens, w_in, table):
    _, rows, width = tokens.shape
    inner = w_in.shape[1]
    shape = lambda n, kind=BF16: jax.ShapeDtypeStruct((steps, rows, n), kind)
    outs = [shape(inner), shape(width), shape(width), shape(width), shape(128, F32)]
    outs += [shape(inner), shape(inner), shape(128, F32)]
    params = [w_in, table]
    return call(
        functools.partial(front_kernel, base),
        win,
        [tokens] + params,
        [per_slot(base, rows, width)] + [whole(p) for p in params],
        outs,
        [per_slot(0, rows, o.shape[2]) for o in outs],
        [],
        steps,
        6 * steps * rows * width * inner,
        steps * rows * width * 12,
        {},
        "front",
    )


def halo(values, hops, axis_size):
    before, after = [], []
    rows = values.shape[1]
    edge = min(rows, REACH)
    for hop in range(1, hops + 1):
        up = [(i, i + hop) for i in range(axis_size - hop)]
        down = [(i + hop, i) for i in range(axis_size - hop)]
        before.insert(0, lax.ppermute(values[:, rows - edge :], "seq", up))
        after.append(lax.ppermute(values[:, :edge], "seq", down))
    return before, after


def rear(win, base, steps, pieces, cot, params, carry, last):
    _, rows, width = cot.shape
    w_conv, w_out, _ = params
    inner = w_conv.shape[2]
    halves = len(pieces) // 2
    first = carry is None
    args = list(pieces) + [cot] + params
    specs = [per_slot(0, p.shape[1], inner) for p in pieces]
    specs += [per_slot(base, rows, width)] + [whole(p) for p in params]
    if not first:
        args += carry
        specs += [whole(c) for c in carry]
    kind = BF16 if last else F32
    outs = [
        jax.ShapeDtypeStruct((steps, rows, inner), BF16),
        jax.ShapeDtypeStruct((steps, rows, inner), BF16),
        jax.ShapeDtypeStruct(w_conv.shape, kind),
        jax.ShapeDtypeStruct(w_out.shape, kind),
        jax.ShapeDtypeStruct((8, width), F32),
    ]
    out_specs = [per_slot(0, rows, inner)] * 2
    out_specs += [whole(o) for o in outs[2:]]
    scratch = [
        pltpu.VMEM(w_conv.shape, F32),
        pltpu.VMEM(w_out.shape, F32),
        pltpu.VMEM((8, width), F32),
        pltpu.VMEM((rows + 2 * REACH, inner), BF16),
    ]
    return call(
        functools.partial(rear_kernel, base, first, last, halves, rows),
        win,
        args,
        specs,
        outs,
        out_specs,
        scratch,
        steps,
        2 * steps * rows * inner * (2 * TAPS * inner + 2 * width),
        steps * rows * width * 6,
        {},
        "rear",
    )


def back(win, base, steps, pieces, tokens, cot, kept, params, carry, last):
    _, rows, width = cot.shape
    w_conv, w_in, _, _ = params
    inner = w_conv.shape[2]
    halves = len(pieces) // 2
    first = carry is None
    args = list(pieces) + [tokens, cot] + list(kept) + params
    specs = [per_slot(0, p.shape[1], inner) for p in pieces]
    specs += [per_slot(base, rows, width)] * 2
    specs += [per_slot(0, rows, k.shape[2]) for k in kept] + [whole(p) for p in params]
    aliases = {}
    if not first:
        args += carry[2:] + carry[:2]
        specs += [whole(c) for c in carry[2:]] + [pl.BlockSpec(memory_space=pl.ANY)] * 2
        aliases = {len(args) - 1: 0, len(args): 1}
    kind = BF16 if last else F32
    outs = [
        jax.ShapeDtypeStruct(cot.shape, BF16),
        jax.ShapeDtypeStruct(cot.shape, BF16),
        jax.ShapeDtypeStruct((w_in.size // 2048, 16, 128) if last else w_in.shape, kind),
        jax.ShapeDtypeStruct((8, width), F32),
    ]
    out_specs = [per_slot(base, rows, width)] * 2 + [whole(o) for o in outs[2:]]
    scratch = [
        pltpu.VMEM(w_in.shape, F32),
        pltpu.VMEM((8, width), F32),
        pltpu.VMEM((rows + 2 * REACH, inner), BF16),
    ]
    return call(
        functools.partial(back_kernel, base, first, last, halves, rows),
        win,
        args,
        specs,
        outs,
        out_specs,
        scratch,
        steps,
        2 * steps * rows * inner * (TAPS * inner + 3 * width),
        steps * rows * width * 17,
        aliases,
        "back",
    )


def sum_kernel(grid_shape, tiles, gw, small_a, small_b, out, small, mine, got, half, got_x, part, got_d, full, sends, recvs):
    d_size, x_size = grid_shape
    seq, dp = lax.axis_index("seq"), lax.axis_index("dp")
    core, x = lax.rem(seq, 2), lax.div(seq, 2)
    sibling = {"seq": seq + 1 - 2 * core}
    x_peers = [{"seq": 2 * lax.rem(x + o, x_size) + core} for o in range(1, x_size)]
    d_peers = [{"dp": lax.rem(dp + o, d_size)} for o in range(1, d_size)]
    peers = [sibling] + x_peers + d_peers
    barrier = pltpu.get_barrier_semaphore()
    for peer in peers:
        pl.semaphore_signal(barrier, inc=1, device_id=peer, device_id_type=pl.DeviceIdType.MESH)
    used = gw.shape[0]
    mine[0:used] = gw[...]
    columns = small_a.shape[1] // 128
    for col in range(columns):
        lanes = slice(col * 128, (col + 1) * 128)
        mine[used + col] = jnp.concatenate([small_a[:, lanes], small_b[:, lanes]], axis=0).astype(
            BF16
        )
    spare = mine.shape[0] - used - columns
    if spare:
        mine[used + columns :] = jnp.zeros((spare, 16, 128), BF16)
    pl.semaphore_wait(barrier, len(peers))
    count = [0]

    def send(src, dst, peer):
        at = count[0]
        count[0] += 1
        copy = pltpu.make_async_remote_copy(
            src_ref=src,
            dst_ref=dst,
            send_sem=sends.at[at],
            recv_sem=recvs.at[at],
            device_id=peer,
            device_id_type=pl.DeviceIdType.MESH,
        )
        copy.start()
        return copy

    x_tiles = d_size * tiles
    core_tiles = x_size * x_tiles
    copies = [send(mine.at[pl.ds((1 - core) * core_tiles, core_tiles)], got, sibling)]
    copies[0].wait_recv()
    half[...] = (
        mine[pl.ds(core * core_tiles, core_tiles)].astype(F32) + got[...].astype(F32)
    ).astype(BF16)
    now = []
    for o, peer in enumerate(x_peers):
        target = lax.rem(x + o + 1, x_size)
        now.append(send(half.at[pl.ds(target * x_tiles, x_tiles)], got_x.at[o], peer))
    for copy in now:
        copy.wait_recv()
    copies += now
    total = half[pl.ds(x * x_tiles, x_tiles)].astype(F32)
    for o in range(x_size - 1):
        total += got_x[o].astype(F32)
    part[...] = total.astype(BF16)
    now = []
    for o, peer in enumerate(d_peers):
        target = lax.rem(dp + o + 1, d_size)
        now.append(send(part.at[pl.ds(target * tiles, tiles)], got_d.at[o], peer))
    for copy in now:
        copy.wait_recv()
    copies += now
    total = part[pl.ds(dp * tiles, tiles)].astype(F32)
    for o in range(d_size - 1):
        total += got_d[o].astype(F32)
    home_x = core * core_tiles + x * x_tiles
    own = pl.ds(home_x + dp * tiles, tiles)
    full[own] = total.astype(BF16)
    for peers, span in (
        (d_peers, own),
        (x_peers, pl.ds(home_x, x_tiles)),
        ([sibling], pl.ds(core * core_tiles, core_tiles)),
    ):
        now = [send(full.at[span], full.at[span], peer) for peer in peers]
        for copy in now:
            copy.wait_recv()
        copies += now
    for copy in copies:
        copy.wait_send()
    depth = out.shape[0] // 16
    for col in range(out.shape[1] // 128):
        piece = full[col * depth : (col + 1) * depth].astype(F32)
        out[:, col * 128 : (col + 1) * 128] = piece.reshape(out.shape[0], 128)
    for col in range(columns):
        small[:, col * 128 : (col + 1) * 128] = full[used + col].astype(F32)


def sum_all(gw, small_a, small_b, shape):
    d_size, x_size = lax.axis_size("dp"), lax.axis_size("seq") // 2
    devices = 2 * d_size * x_size
    tiles = -(-(gw.shape[0] + small_a.shape[1] // 128) // devices)
    x_tiles = d_size * tiles
    copies = 2 * (1 + x_size - 1 + d_size - 1)
    block = lambda *lead: pltpu.VMEM((*lead, 16, 128), BF16)
    return pl.pallas_call(
        functools.partial(sum_kernel, (d_size, x_size), tiles),
        out_shape=[
            jax.ShapeDtypeStruct(shape, F32),
            jax.ShapeDtypeStruct((16, small_a.shape[1]), F32),
        ],
        in_specs=[pl.BlockSpec(memory_space=pltpu.VMEM)] * 3,
        out_specs=[pl.BlockSpec(memory_space=pltpu.VMEM)] * 2,
        scratch_shapes=[
            block(devices * tiles),
            block(x_size * x_tiles),
            block(x_size * x_tiles),
            block(x_size - 1, x_tiles),
            block(x_tiles),
            block(d_size - 1, tiles),
            block(devices * tiles),
            pltpu.SemaphoreType.DMA((copies,)),
            pltpu.SemaphoreType.DMA((copies,)),
        ],
        compiler_params=pltpu.CompilerParams(collective_id=0, has_side_effects=True),
        cost_estimate=pl.CostEstimate(flops=0, bytes_accessed=120_000_000, transcendentals=0),
        name="sum_all",
    )(gw, small_a, small_b)


def body(
    tokens,
    cotangent,
    ln1_gain,
    ln1_bias,
    w_in,
    b_in,
    ln2_gain,
    ln2_bias,
    w_conv,
    b_conv,
    ln3_gain,
    ln3_bias,
    w_out,
    b_out,
    lengths,
    offsets,
    live,
):
    axis_size = lax.axis_size("seq")
    slots, rows, width = tokens.shape
    inner = w_in.shape[1]
    hops = -(-REACH // rows)
    begin = lax.axis_index("seq") * rows
    filled = jnp.arange(slots, dtype=jnp.int32) < live[0]
    low = jnp.clip(offsets - begin, 0, rows)
    high = jnp.where(filled, jnp.clip(offsets + lengths - begin, 0, rows), 0)
    win = jnp.stack([low, high])
    table = jnp.stack(
        [
            jnp.pad(v.astype(F32), (0, width - v.shape[0]))
            for v in (ln1_gain, ln1_bias, b_in, ln2_gain, ln2_bias, b_conv, ln3_gain, ln3_bias, b_out)
        ]
    )
    chunks = 2
    steps = slots // chunks
    fronts = [
        front(win, c * steps, steps, tokens, w_in, table)
        for c in range(chunks)
    ]
    carry = None
    grads, kept = [], []
    params = [w_conv, w_out, table]
    for c in range(chunks):
        before, after = halo(fronts[c][0], hops, axis_size)
        pieces = before + [fronts[c][0]] + after
        res = rear(
            win, c * steps, steps, pieces, cotangent, params, carry, c == chunks - 1
        )
        kept.append(list(fronts[c][1:]) + [res[0]])
        grads.append(res[1])
        carry = list(res[2:])
    gw_conv, gw_out = lax.psum(tuple(carry[:2]), ("dp", "seq"))
    small_rear = carry[2]
    carry = None
    params = [w_conv, w_in, w_out, table]
    for c in range(chunks):
        before, after = halo(grads[c], hops, axis_size)
        pieces = before + [grads[c]] + after
        res = back(
            win, c * steps, steps, pieces, tokens, cotangent, kept[c], params, carry, c == chunks - 1
        )
        carry = list(res)
    output, grad_tokens = carry[:2]
    gw_in, smalls = sum_all(carry[2], small_rear, carry[3], w_in.shape)
    small_rear, small_back = smalls[:8], smalls[8:]
    return (
        output,
        grad_tokens,
        small_back[0],
        small_back[1],
        gw_in,
        small_back[3, :inner],
        small_back[2, :inner],
        small_back[2, inner : 2 * inner],
        gw_conv.astype(F32),
        small_rear[2, :inner],
        small_rear[1, :inner],
        small_rear[1, inner : 2 * inner],
        gw_out.astype(F32),
        small_rear[0],
    )


def solution(mesh):
    return jax.shard_map(
        body,
        mesh=mesh,
        in_specs=(P("dp", "seq", None),) * 2 + (P(),) * 12 + (P("dp"),) * 3,
        out_specs=(P("dp", "seq", None),) * 2 + (P(),) * 12,
        check_vma=False,
    )
```

```python
import functools

import jax
import jax.numpy as jnp
from jax import lax
from jax.experimental import pallas as pl
from jax.experimental.pallas import tpu as pltpu
from jax.sharding import PartitionSpec as P

TAPS = 5
STEP = 128
REACH = (TAPS - 1) // 2 * STEP
EPSILON = 1e-05
ROOT_TWO = 1.4142135623730951
EXP_SCALE = -2.8853900817779268
INV_ROOT_TAU = 0.3989422804014327
G1, B1, BIN, G2, B2, BCONV, G3, B3, BOUT = range(9)
VMEM_LIMIT = 60 * 1024 * 1024
F32 = jnp.float32
BF16 = jnp.bfloat16


def dot(left, right):
    return jnp.dot(left, right, preferred_element_type=F32)


def dot_back(left, right):
    return lax.dot_general(left, right, (((1,), (1,)), ((), ())), preferred_element_type=F32)


def dot_rows(left, right):
    return lax.dot_general(left, right, (((0,), (0,)), ((), ())), preferred_element_type=F32)


def normalize(values):
    centre = values - jnp.mean(values, axis=-1, keepdims=True)
    inv = lax.rsqrt(jnp.mean(centre * centre, axis=-1, keepdims=True) + EPSILON)
    return centre * inv, inv


def gelu_parts(half):
    rise = 1.0 + lax.erf(half * ROOT_TWO)
    return half * rise, rise


def slope_of(half, rise):
    return 0.5 * rise + half * (2.0 * INV_ROOT_TAU * jnp.exp2((half * half) * EXP_SCALE))


def gelu_pair(half):
    act, rise = gelu_parts(half)
    return act, slope_of(half, rise)


def norm_back(grad, normed, inv, gain):
    scaled = grad * gain
    return inv * (
        scaled
        - jnp.mean(scaled, axis=-1, keepdims=True)
        - normed * jnp.mean(scaled * normed, axis=-1, keepdims=True)
    )


def keep_rows(win_ref, slot, shape):
    rows = lax.broadcasted_iota(jnp.int32, shape, 0)
    return (rows >= win_ref[0, slot]) & (rows < win_ref[1, slot])


def row_sum(values):
    return jnp.sum(values, axis=0, keepdims=True)


def spread(inv):
    return jnp.broadcast_to(inv, (inv.shape[0], 128))


def front_kernel(base, win, tok, w_in, table, h, a1, n1, r1, s2, n2, r2):
    slot = base + pl.program_id(0)
    inner = w_in.shape[1]
    g1, b1 = table[G1 : G1 + 1], table[B1 : B1 + 1]
    g2, b2 = table[G2 : G2 + 1, :inner], table[B2 : B2 + 1, :inner]
    b_in = table[BIN : BIN + 1, :inner]
    active = win[1, slot] > win[0, slot]

    @pl.when(active)
    def _():
        normed, inv = normalize(tok[0].astype(F32))
        n1[0] = normed.astype(BF16)
        r1[0] = spread(inv)
        act, _ = gelu_parts(normed * (0.5 * g1) + 0.5 * b1)
        act = act.astype(BF16)
        a1[0] = act
        hidden = dot(act, w_in[...]) + b_in
        normed, inv = normalize(hidden)
        n2[0] = normed.astype(BF16)
        r2[0] = spread(inv)
        act, slope = gelu_pair(normed * (0.5 * g2) + 0.5 * b2)
        s2[0] = slope.astype(BF16)
        h[0] = jnp.where(keep_rows(win, slot, act.shape), act, 0.0).astype(BF16)

    @pl.when(jnp.logical_not(active))
    def _():
        h[0] = jnp.zeros(h.shape[1:], BF16)


def rear_kernel(
    base, first, last, halves, rows, win, *refs
):
    pieces = refs[: 2 * halves + 1]
    refs = refs[2 * halves + 1 :]
    cot, w_conv, w_out, table = refs[:4]
    refs = refs[4:]
    if not first:
        wconv_in, wout_in, small_in = refs[:3]
        refs = refs[3:]
    a3, dc_out, gw_conv, gw_out, small, acc_conv, acc_out, acc_small, strip = refs
    step = pl.program_id(0)

    @pl.when(step == 0)
    def _():
        if first:
            acc_conv[...] = jnp.zeros_like(acc_conv)
            acc_out[...] = jnp.zeros_like(acc_out)
            acc_small[...] = jnp.zeros_like(acc_small)
        else:
            acc_conv[...] = wconv_in[...]
            acc_out[...] = wout_in[...]
            acc_small[...] = small_in[...]

    slot = base + step
    at = 0
    for piece in pieces:
        count = piece.shape[1]
        strip[at : at + count] = piece[0]
        at += count
    inner = strip.shape[1]
    g3, b3 = table[G3 : G3 + 1, :inner], table[B3 : B3 + 1, :inner]
    b_conv = table[BCONV : BCONV + 1, :inner]

    taps = jnp.concatenate([strip[tap * STEP : tap * STEP + rows] for tap in range(TAPS)], axis=1)
    conv = dot(taps, w_conv[...].reshape(TAPS * inner, inner))
    conv = (conv + b_conv).astype(BF16).astype(F32)
    normed, inv = normalize(conv)
    act, slope = gelu_pair(normed * (0.5 * g3) + 0.5 * b3)
    act = act.astype(BF16)
    a3[0] = act
    active = win[1, slot] > win[0, slot]

    @pl.when(active)
    def _():
        gy = jnp.where(keep_rows(win, slot, cot.shape[1:]), cot[0].astype(F32), 0.0)
        acc_small[0:1] += row_sum(gy)
        gy = gy.astype(BF16)
        acc_out[...] += dot_rows(act, gy)
        grad = dot_back(gy, w_out[...]) * slope
        acc_small[1:2, 0:inner] += row_sum(grad * normed)
        acc_small[1:2, inner : 2 * inner] += row_sum(grad)
        dc = norm_back(grad, normed, inv, g3).astype(BF16)
        dc_out[0] = dc
        acc_small[2:3, 0:inner] += row_sum(dc.astype(F32))
        for tap in range(TAPS):
            acc_conv[tap] += dot_rows(strip[tap * STEP : tap * STEP + rows], dc)

    @pl.when(jnp.logical_not(active))
    def _():
        dc_out[0] = jnp.zeros(dc_out.shape[1:], BF16)

    @pl.when(step == pl.num_programs(0) - 1)
    def _():
        kind = BF16 if last else F32
        gw_conv[...] = acc_conv[...].astype(kind)
        gw_out[...] = acc_out[...].astype(kind)
        small[...] = acc_small[...]


def back_kernel(base, first, last, halves, rows, win, *refs):
    pieces = refs[: 2 * halves + 1]
    refs = refs[2 * halves + 1 :]
    tok, cot, a1, n1, r1, s2, n2, r2, a3, w_conv, w_in, w_out, table = refs[:13]
    refs = refs[13:]
    if not first:
        win_in, small_in = refs[:2]
        refs = refs[4:]
    out, grad_out, gw_in, small, acc_in, acc_small, strip, w_flat, slopes = refs
    step = pl.program_id(0)

    @pl.when(step == 0)
    def _():
        for tap in range(TAPS):
            w_flat[:, tap * strip.shape[1] : (tap + 1) * strip.shape[1]] = w_conv[tap]
        if first:
            acc_in[...] = jnp.zeros_like(acc_in)
            acc_small[...] = jnp.zeros_like(acc_small)
        else:
            acc_in[...] = win_in[...]
            acc_small[...] = small_in[...]

    slot = base + step
    at = 0
    for piece in pieces:
        count = piece.shape[1]
        strip[at : at + count] = piece[0]
        at += count
    inner = strip.shape[1]
    g1, g2 = table[G1 : G1 + 1], table[G2 : G2 + 1, :inner]
    b1 = table[B1 : B1 + 1]
    width = cot.shape[2]

    def residual():
        sent = dot(a3[0], w_out[...]) + table[BOUT : BOUT + 1]
        out[0] = (tok[0].astype(F32) + sent).astype(BF16)

    active = win[1, slot] > win[0, slot]

    @pl.when(active)
    def _():
        residual()
        half = n1[0].astype(F32) * (0.5 * g1) + 0.5 * b1
        slopes[...] = slope_of(half, 1.0 + lax.erf(half * ROOT_TWO))
        begins = [2 * REACH - tap * STEP for tap in range(TAPS)]
        taps = jnp.concatenate([strip[at : at + rows] for at in begins], axis=1)
        dh = dot_back(taps, w_flat[...])
        dh = jnp.where(keep_rows(win, slot, dh.shape), dh, 0.0).astype(BF16).astype(F32)
        grad = dh * s2[0].astype(F32)
        normed = n2[0].astype(F32)
        acc_small[2:3, 0:inner] += row_sum(grad * normed)
        acc_small[2:3, inner : 2 * inner] += row_sum(grad)
        inv = jnp.concatenate([r2[0]] * (inner // 128), axis=-1)
        dz = norm_back(grad, normed, inv, g2).astype(BF16)
        acc_small[3:4, 0:inner] += row_sum(dz.astype(F32))
        acc_in[...] += dot_rows(a1[0], dz)
        grad = dot_back(dz, w_in[...]) * slopes[...]
        normed = n1[0].astype(F32)
        acc_small[0:1] += row_sum(grad * normed)
        acc_small[1:2] += row_sum(grad)
        inv = jnp.concatenate([r1[0]] * (width // 128), axis=-1)
        branch = norm_back(grad, normed, inv, g1)
        gy = jnp.where(keep_rows(win, slot, cot.shape[1:]), cot[0].astype(F32), 0.0)
        grad_out[0] = (gy + branch).astype(BF16)

    @pl.when(jnp.logical_not(active))
    def _():
        residual()
        grad_out[0] = jnp.zeros(grad_out.shape[1:], BF16)

    @pl.when(step == pl.num_programs(0) - 1)
    def _():
        if last:
            depth = acc_in.shape[0] // 16
            for col in range(inner // 128):
                part = acc_in[:, col * 128 : (col + 1) * 128].reshape(depth, 16, 128)
                gw_in[col * depth : (col + 1) * depth] = part.astype(BF16)
        else:
            gw_in[...] = acc_in[...]
        small[...] = acc_small[...]


def whole(array):
    rank = array.ndim
    return pl.BlockSpec(array.shape, lambda i, w: (0,) * rank, pipeline_mode=pl.Buffered(1))


def per_slot(base, rows, width):
    return pl.BlockSpec((1, rows, width), lambda i, w: (base + i, 0, 0))


def call(kernel, win, args, specs, outs, out_specs, scratch, steps, flops, cost_bytes, aliases, name):
    return pl.pallas_call(
        kernel,
        out_shape=outs,
        grid_spec=pltpu.PrefetchScalarGridSpec(
            num_scalar_prefetch=1,
            grid=(steps,),
            in_specs=specs,
            out_specs=out_specs,
            scratch_shapes=scratch,
        ),
        compiler_params=pltpu.CompilerParams(
            dimension_semantics=("arbitrary",), vmem_limit_bytes=VMEM_LIMIT
        ),
        cost_estimate=pl.CostEstimate(
            flops=flops, bytes_accessed=cost_bytes, transcendentals=0
        ),
        input_output_aliases=aliases,
        name=name,
    )(win, *args)


def front(win, base, steps, tokens, w_in, table):
    _, rows, width = tokens.shape
    inner = w_in.shape[1]
    shape = lambda n, kind=BF16: jax.ShapeDtypeStruct((steps, rows, n), kind)
    outs = [shape(inner), shape(width), shape(width), shape(128, F32)]
    outs += [shape(inner), shape(inner), shape(128, F32)]
    params = [w_in, table]
    return call(
        functools.partial(front_kernel, base),
        win,
        [tokens] + params,
        [per_slot(base, rows, width)] + [whole(p) for p in params],
        outs,
        [per_slot(0, rows, o.shape[2]) for o in outs],
        [],
        steps,
        6 * steps * rows * width * inner,
        steps * rows * width * 12,
        {},
        "front",
    )


def halo(values, hops, axis_size):
    before, after = [], []
    rows = values.shape[1]
    edge = min(rows, REACH)
    for hop in range(1, hops + 1):
        up = [(i, i + hop) for i in range(axis_size - hop)]
        down = [(i + hop, i) for i in range(axis_size - hop)]
        before.insert(0, lax.ppermute(values[:, rows - edge :], "seq", up))
        after.append(lax.ppermute(values[:, :edge], "seq", down))
    return before, after


def rear(win, base, steps, pieces, cot, params, carry, last):
    _, rows, width = cot.shape
    w_conv, w_out, _ = params
    inner = w_conv.shape[2]
    halves = len(pieces) // 2
    first = carry is None
    args = list(pieces) + [cot] + params
    specs = [per_slot(0, p.shape[1], inner) for p in pieces]
    specs += [per_slot(base, rows, width)] + [whole(p) for p in params]
    if not first:
        args += carry
        specs += [whole(c) for c in carry]
    kind = BF16 if last else F32
    outs = [
        jax.ShapeDtypeStruct((steps, rows, inner), BF16),
        jax.ShapeDtypeStruct((steps, rows, inner), BF16),
        jax.ShapeDtypeStruct(w_conv.shape, kind),
        jax.ShapeDtypeStruct(w_out.shape, kind),
        jax.ShapeDtypeStruct((8, width), F32),
    ]
    out_specs = [per_slot(0, rows, inner)] * 2
    out_specs += [whole(o) for o in outs[2:]]
    scratch = [
        pltpu.VMEM(w_conv.shape, F32),
        pltpu.VMEM(w_out.shape, F32),
        pltpu.VMEM((8, width), F32),
        pltpu.VMEM((rows + 2 * REACH, inner), BF16),
    ]
    return call(
        functools.partial(rear_kernel, base, first, last, halves, rows),
        win,
        args,
        specs,
        outs,
        out_specs,
        scratch,
        steps,
        2 * steps * rows * inner * (2 * TAPS * inner + 2 * width),
        steps * rows * width * 6,
        {},
        "rear",
    )


def back(win, base, steps, pieces, tokens, cot, kept, params, carry, last):
    _, rows, width = cot.shape
    w_conv, w_in, _, _ = params
    inner = w_conv.shape[2]
    halves = len(pieces) // 2
    first = carry is None
    args = list(pieces) + [tokens, cot] + list(kept) + params
    specs = [per_slot(0, p.shape[1], inner) for p in pieces]
    specs += [per_slot(base, rows, width)] * 2
    specs += [per_slot(0, rows, k.shape[2]) for k in kept] + [whole(p) for p in params]
    aliases = {}
    if not first:
        args += carry[2:] + carry[:2]
        specs += [whole(c) for c in carry[2:]] + [pl.BlockSpec(memory_space=pl.ANY)] * 2
        aliases = {len(args) - 1: 0, len(args): 1}
    kind = BF16 if last else F32
    outs = [
        jax.ShapeDtypeStruct(cot.shape, BF16),
        jax.ShapeDtypeStruct(cot.shape, BF16),
        jax.ShapeDtypeStruct((w_in.size // 2048, 16, 128) if last else w_in.shape, kind),
        jax.ShapeDtypeStruct((8, width), F32),
    ]
    out_specs = [per_slot(base, rows, width)] * 2 + [whole(o) for o in outs[2:]]
    scratch = [
        pltpu.VMEM(w_in.shape, F32),
        pltpu.VMEM((8, width), F32),
        pltpu.VMEM((rows + 2 * REACH, inner), BF16),
        pltpu.VMEM((inner, TAPS * inner), BF16),
        pltpu.VMEM((rows, width), F32),
    ]
    return call(
        functools.partial(back_kernel, base, first, last, halves, rows),
        win,
        args,
        specs,
        outs,
        out_specs,
        scratch,
        steps,
        2 * steps * rows * inner * (TAPS * inner + 3 * width),
        steps * rows * width * 17,
        aliases,
        "back",
    )


def sum_kernel(grid_shape, tiles, gw, small_a, small_b, out, small, mine, got, half, got_x, part, got_d, full, sends, recvs):
    d_size, x_size = grid_shape
    seq, dp = lax.axis_index("seq"), lax.axis_index("dp")
    core, x = lax.rem(seq, 2), lax.div(seq, 2)
    sibling = {"seq": seq + 1 - 2 * core}
    x_peers = [{"seq": 2 * lax.rem(x + o, x_size) + core} for o in range(1, x_size)]
    d_peers = [{"dp": lax.rem(dp + o, d_size)} for o in range(1, d_size)]
    peers = [sibling] + x_peers + d_peers
    barrier = pltpu.get_barrier_semaphore()
    for peer in peers:
        pl.semaphore_signal(barrier, inc=1, device_id=peer, device_id_type=pl.DeviceIdType.MESH)
    used = gw.shape[0]
    mine[0:used] = gw[...]
    columns = small_a.shape[1] // 128
    for col in range(columns):
        lanes = slice(col * 128, (col + 1) * 128)
        mine[used + col] = jnp.concatenate([small_a[:, lanes], small_b[:, lanes]], axis=0).astype(
            BF16
        )
    spare = mine.shape[0] - used - columns
    if spare:
        mine[used + columns :] = jnp.zeros((spare, 16, 128), BF16)
    pl.semaphore_wait(barrier, len(peers))
    count = [0]

    def send(src, dst, peer):
        at = count[0]
        count[0] += 1
        copy = pltpu.make_async_remote_copy(
            src_ref=src,
            dst_ref=dst,
            send_sem=sends.at[at],
            recv_sem=recvs.at[at],
            device_id=peer,
            device_id_type=pl.DeviceIdType.MESH,
        )
        copy.start()
        return copy

    x_tiles = d_size * tiles
    core_tiles = x_size * x_tiles
    copies = [send(mine.at[pl.ds((1 - core) * core_tiles, core_tiles)], got, sibling)]
    copies[0].wait_recv()
    half[...] = (
        mine[pl.ds(core * core_tiles, core_tiles)].astype(F32) + got[...].astype(F32)
    ).astype(BF16)
    now = []
    for o, peer in enumerate(x_peers):
        target = lax.rem(x + o + 1, x_size)
        now.append(send(half.at[pl.ds(target * x_tiles, x_tiles)], got_x.at[o], peer))
    for copy in now:
        copy.wait_recv()
    copies += now
    total = half[pl.ds(x * x_tiles, x_tiles)].astype(F32)
    for o in range(x_size - 1):
        total += got_x[o].astype(F32)
    part[...] = total.astype(BF16)
    now = []
    for o, peer in enumerate(d_peers):
        target = lax.rem(dp + o + 1, d_size)
        now.append(send(part.at[pl.ds(target * tiles, tiles)], got_d.at[o], peer))
    for copy in now:
        copy.wait_recv()
    copies += now
    total = part[pl.ds(dp * tiles, tiles)].astype(F32)
    for o in range(d_size - 1):
        total += got_d[o].astype(F32)
    home_x = core * core_tiles + x * x_tiles
    own = pl.ds(home_x + dp * tiles, tiles)
    full[own] = total.astype(BF16)
    for peers, span in (
        (d_peers, own),
        (x_peers, pl.ds(home_x, x_tiles)),
        ([sibling], pl.ds(core * core_tiles, core_tiles)),
    ):
        now = [send(full.at[span], full.at[span], peer) for peer in peers]
        for copy in now:
            copy.wait_recv()
        copies += now
    for copy in copies:
        copy.wait_send()
    depth = out.shape[0] // 16
    for col in range(out.shape[1] // 128):
        piece = full[col * depth : (col + 1) * depth].astype(F32)
        out[:, col * 128 : (col + 1) * 128] = piece.reshape(out.shape[0], 128)
    for col in range(columns):
        small[:, col * 128 : (col + 1) * 128] = full[used + col].astype(F32)


def sum_all(gw, small_a, small_b, shape):
    d_size, x_size = lax.axis_size("dp"), lax.axis_size("seq") // 2
    devices = 2 * d_size * x_size
    tiles = -(-(gw.shape[0] + small_a.shape[1] // 128) // devices)
    x_tiles = d_size * tiles
    copies = 2 * (1 + x_size - 1 + d_size - 1)
    block = lambda *lead: pltpu.VMEM((*lead, 16, 128), BF16)
    return pl.pallas_call(
        functools.partial(sum_kernel, (d_size, x_size), tiles),
        out_shape=[
            jax.ShapeDtypeStruct(shape, F32),
            jax.ShapeDtypeStruct((16, small_a.shape[1]), F32),
        ],
        in_specs=[pl.BlockSpec(memory_space=pltpu.VMEM)] * 3,
        out_specs=[pl.BlockSpec(memory_space=pltpu.VMEM)] * 2,
        scratch_shapes=[
            block(devices * tiles),
            block(x_size * x_tiles),
            block(x_size * x_tiles),
            block(x_size - 1, x_tiles),
            block(x_tiles),
            block(d_size - 1, tiles),
            block(devices * tiles),
            pltpu.SemaphoreType.DMA((copies,)),
            pltpu.SemaphoreType.DMA((copies,)),
        ],
        compiler_params=pltpu.CompilerParams(collective_id=0, has_side_effects=True),
        cost_estimate=pl.CostEstimate(flops=0, bytes_accessed=120_000_000, transcendentals=0),
        name="sum_all",
    )(gw, small_a, small_b)


def body(
    tokens,
    cotangent,
    ln1_gain,
    ln1_bias,
    w_in,
    b_in,
    ln2_gain,
    ln2_bias,
    w_conv,
    b_conv,
    ln3_gain,
    ln3_bias,
    w_out,
    b_out,
    lengths,
    offsets,
    live,
):
    axis_size = lax.axis_size("seq")
    slots, rows, width = tokens.shape
    inner = w_in.shape[1]
    hops = -(-REACH // rows)
    begin = lax.axis_index("seq") * rows
    filled = jnp.arange(slots, dtype=jnp.int32) < live[0]
    low = jnp.clip(offsets - begin, 0, rows)
    high = jnp.where(filled, jnp.clip(offsets + lengths - begin, 0, rows), 0)
    win = jnp.stack([low, high])
    table = jnp.stack(
        [
            jnp.pad(v.astype(F32), (0, width - v.shape[0]))
            for v in (ln1_gain, ln1_bias, b_in, ln2_gain, ln2_bias, b_conv, ln3_gain, ln3_bias, b_out)
        ]
    )
    chunks = 2
    steps = slots // chunks
    fronts = [
        front(win, c * steps, steps, tokens, w_in, table)
        for c in range(chunks)
    ]
    carry = None
    grads, kept = [], []
    params = [w_conv, w_out, table]
    for c in range(chunks):
        before, after = halo(fronts[c][0], hops, axis_size)
        pieces = before + [fronts[c][0]] + after
        res = rear(
            win, c * steps, steps, pieces, cotangent, params, carry, c == chunks - 1
        )
        kept.append(list(fronts[c][1:]) + [res[0]])
        grads.append(res[1])
        carry = list(res[2:])
    gw_conv, gw_out = lax.psum(tuple(carry[:2]), ("dp", "seq"))
    small_rear = carry[2]
    carry = None
    params = [w_conv, w_in, w_out, table]
    for c in range(chunks):
        before, after = halo(grads[c], hops, axis_size)
        pieces = before + [grads[c]] + after
        res = back(
            win, c * steps, steps, pieces, tokens, cotangent, kept[c], params, carry, c == chunks - 1
        )
        carry = list(res)
    output, grad_tokens = carry[:2]
    gw_in, smalls = sum_all(carry[2], small_rear, carry[3], w_in.shape)
    small_rear, small_back = smalls[:8], smalls[8:]
    return (
        output,
        grad_tokens,
        small_back[0],
        small_back[1],
        gw_in,
        small_back[3, :inner],
        small_back[2, :inner],
        small_back[2, inner : 2 * inner],
        gw_conv.astype(F32),
        small_rear[2, :inner],
        small_rear[1, :inner],
        small_rear[1, inner : 2 * inner],
        gw_out.astype(F32),
        small_rear[0],
    )


def solution(mesh):
    return jax.shard_map(
        body,
        mesh=mesh,
        in_specs=(P("dp", "seq", None),) * 2 + (P(),) * 12 + (P("dp"),) * 3,
        out_specs=(P("dp", "seq", None),) * 2 + (P(),) * 12,
        check_vma=False,
    )
```
